32 devices in a mesh: pair: 8 (over y, x, core), grp: 4 (over z).
Axes of the slice: x: 2, y: 2, z: 4, core: 2. Of those that a mesh axis runs over, the one named last changes fastest.
Arguments:
- sector_rows: int32 [4], replicated, may hold values from 1 to 256, 768 in all
- wavefunction: bfloat16 [4, 256, 512], P('grp'), may hold values from -6 to 6
- left_ops: bfloat16 [64, 4, 256, 256], P(('pair', 'grp')), may hold values from -0.375 to 0.375
- right_diag: bfloat16 [64, 4, 512], P('pair', 'grp'), may hold values from -0.0078125 to 0.0078125
Outputs:
- slab: float32 [64, 64], P(('pair', 'grp'))
The draws below stay inside these ranges and needn't reach their ends.
Inputs may be any that keep to these rules, and one draw needn't show every extreme that they name: `sector_rows`: each entry counts the live leading rows of one sector block; at least one sector has 256.
All inputs are finite; a program needn't handle non-finite values.
Results may differ from the reference program's by a relative error of at most 0.0029.
Values may be sent and summed in bfloat16 or wider, within the bound.
No kernel may reach another device: no remote copies, remote signals or barrier semaphores. Data moves between devices by JAX's collectives and lax.ppermute only.
A program may use at most 64 MiB of HBM per device.

```python
import math
import jax
import jax.numpy as jnp
import numpy as np
from jax import lax

BLK = 256
RS = 512
Q = 64
NSEC = 4
P_SIZE = 64


def shard_levels(rng, dims, split, least, largest):
    def one(dim, parts):
        draws = jax.random.uniform(jax.random.fold_in(jax.random.fold_in(rng, 6), dim), (parts,), jnp.float32, least / len(split), largest / len(split))
        return jnp.repeat(jnp.exp(draws), dims[dim] // parts).reshape((-1,) + (1,) * (len(dims) - dim - 1))

    level = one(*split[0])
    for cut in split[1:]:
        level = level * one(*cut)
    return level


def length_profile(count, total, bound, skew):
    weights = [(1 << 20) // math.isqrt(standing ** skew) + 1 for standing in range(2, count + 1)]
    spare, counts = total - bound - (count - 1), [1] * (count - 1)
    while spare > 0:
        candidates = [i for i in range(count - 1) if counts[i] < bound]
        whole, budget = sum([weights[i] for i in candidates]), spare
        for i in candidates:
            more = min(bound - counts[i], max(1, budget * weights[i] // whole), spare)
            counts[i] = counts[i] + more
            spare = spare - more
    return np.array([bound] + counts)


def ragged(own_key, amount, total, limit, skew):
    if amount == 2:
        one = jax.random.randint(own_key, (), max(1, total - limit), min(limit, total - 1) + 1)
        return jnp.stack([one, total - one])
    tallies = jnp.asarray(length_profile(amount, total, limit, skew), jnp.int32)
    pairs = (amount - 1) // 2
    donor, receiver = tallies[1:1 + 2 * pairs:2], tallies[2:2 + 2 * pairs:2]
    room = jnp.minimum(donor - 1, limit - receiver)
    shifted = jax.random.randint(jax.random.fold_in(own_key, 1), (pairs,), 0, 1 << 20) % (room + 1)
    tallies = tallies.at[1:1 + 2 * pairs:2].set(donor - shifted).at[2:2 + 2 * pairs:2].set(receiver + shifted)
    return tallies[jax.random.permutation(jax.random.fold_in(own_key, 2), amount)]


def centred(key, extent, scale, most, shards=(), kind=jnp.bfloat16):
    loudness = shard_levels(key, extent, shards, -0.22, 0.18) if shards else 1.0
    result = jax.random.normal(key, extent, jnp.float32) * scale * loudness
    return jnp.minimum(jnp.maximum(result, -most), most).astype(kind)


def setup_inputs(seed: int = 0) -> dict:
    arg_keys = jax.random.split(jax.random.key(seed), 5)
    sector_rows = ragged(arg_keys[0], NSEC, NSEC * BLK * 3 // 4, BLK, 1).astype(jnp.int32)
    wavefunction = centred(arg_keys[1], (NSEC, BLK, RS), 1.0, 6.0, ((0, 4),))
    left_ops = centred(arg_keys[2], (P_SIZE, NSEC, BLK, BLK), BLK ** -0.5, 0.375, ((0, 32),))
    right_diag = centred(arg_keys[3], (Q, NSEC, RS), (NSEC * RS * BLK) ** -0.5, 0.0078125, ((0, 8), (1, 4)))
    return dict(sector_rows=sector_rows, wavefunction=wavefunction, left_ops=left_ops, right_diag=right_diag)


def live_states(sector_rows, wavefunction):
    row_index = lax.broadcasted_iota(jnp.int32, wavefunction.shape, 1)
    return jnp.where(row_index < sector_rows.astype(jnp.int32)[:, None, None], wavefunction, jnp.zeros_like(wavefunction))


def reference(sector_rows, wavefunction, left_ops, right_diag):
    live = live_states(sector_rows, wavefunction)
    live_wide = live.astype(jnp.float32)

    def one_pair(operator_block):
        image = jnp.einsum('sab,sbc->sac', operator_block.astype(jnp.float32), live_wide)
        return jnp.sum(live_wide * image, axis=1)

    weights = lax.map(one_pair, left_ops).astype(jnp.bfloat16)
    flat = weights.reshape(weights.shape[0], -1)
    diag_flat = right_diag.reshape(right_diag.shape[0], -1)
    return lax.dot_general(flat, diag_flat, (((1,), (1,)), ((), ())), preferred_element_type=jnp.float32)
```

```python
import functools

import jax
import jax.numpy as jnp
from jax import lax
from jax.experimental import pallas as pl
from jax.experimental.pallas import tpu as pltpu
from jax.sharding import PartitionSpec as P

LANES = 128
CORES = 2
BOTH = ("pair", "grp")


class Plan:
    def __init__(self, pairs, groups, wave, diag, ops):
        self.pairs, self.groups = pairs, groups
        self.chips = pairs // CORES
        self.rows, self.cols = wave.shape[1], wave.shape[2]
        self.tiles = self.cols // LANES
        self.col_cuts = min(self.chips, self.tiles)
        self.row_cuts = self.chips // self.col_cuts
        self.width = self.cols // self.col_cuts
        self.wide = self.width // LANES
        self.half = self.rows // CORES
        self.piece = self.half // self.row_cuts
        self.diag_rows = diag.shape[0]
        self.live_rows = self.piece * self.wide
        self.tail = self.diag_rows * self.tiles
        self.message = self.live_rows + self.tail
        self.own_pairs = ops.shape[0]

    def batches(self):
        steps = [d for d in range(1, self.groups)]
        near = [d for d in steps if d in (1, self.groups - 1)]
        far = [d for d in steps if d not in near]
        return [b for b in (near, far) if b]


def cut_kernel(plan, rows_ref, wave_ref, diag_ref, out_ref, held, sem):
    me, grp = lax.axis_index("pair"), lax.axis_index("grp")
    core, chip = lax.rem(me, CORES), lax.div(me, CORES)
    col, row = lax.rem(chip, plan.col_cuts), lax.div(chip, plan.col_cuts)
    first = core * plan.half + row * plan.piece
    copy = pltpu.make_async_copy(
        wave_ref.at[
            0,
            pl.ds(pl.multiple_of(first, plan.piece), plan.piece),
            pl.ds(pl.multiple_of(col * plan.width, LANES), plan.width),
        ],
        held,
        sem,
    )
    copy.start()
    diag = diag_ref[:, 0, :]
    for k in range(plan.tiles):
        at = plan.live_rows + k * plan.diag_rows
        out_ref[at : at + plan.diag_rows, :] = diag[:, k * LANES : (k + 1) * LANES]
    limit = rows_ref[grp] - first
    copy.wait()
    index = lax.broadcasted_iota(jnp.int32, held.shape, 0)
    live = jnp.where(index < limit, held[...].astype(jnp.float32), 0.0).astype(jnp.bfloat16)
    for k in range(plan.wide):
        out_ref[k * plan.piece : (k + 1) * plan.piece, :] = live[:, k * LANES : (k + 1) * LANES]


def cut(plan, sector_rows, wave, diag):
    return pl.pallas_call(
        functools.partial(cut_kernel, plan),
        out_shape=jax.ShapeDtypeStruct((plan.message, LANES), jnp.bfloat16),
        in_specs=[
            pl.BlockSpec(memory_space=pltpu.SMEM),
            pl.BlockSpec(memory_space=pl.ANY),
            pl.BlockSpec(memory_space=pltpu.VMEM),
        ],
        out_specs=pl.BlockSpec(memory_space=pltpu.VMEM),
        scratch_shapes=[
            pltpu.VMEM((plan.piece, plan.width), jnp.bfloat16),
            pltpu.SemaphoreType.DMA,
        ],
        name="cut",
    )(sector_rows, wave, diag)


def slab_kernel(plan, batches, rows_ref, wave_ref, ops_ref, *refs):
    count = len(batches)
    mine, theirs = refs[:count], refs[count : 2 * count]
    out_ref, state, diag, weight = refs[2 * count :]
    me, grp = lax.axis_index("pair"), lax.axis_index("grp")
    core, chip = lax.rem(me, CORES), lax.div(me, CORES)
    cols, dr = plan.cols, plan.diag_rows

    weight[...] = jnp.zeros_like(weight)

    def weigh(slot, sector, live):
        wide = live.astype(jnp.float32)
        for p in range(plan.own_pairs):
            image = jnp.dot(ops_ref[p, sector], live, preferred_element_type=jnp.float32)
            total = jnp.sum(wide * image, axis=0, keepdims=True)
            weight[p : p + 1, slot * cols : (slot + 1) * cols] = total

    index = lax.broadcasted_iota(jnp.int32, wave_ref.shape[1:], 0)
    own = jnp.where(index < rows_ref[grp], wave_ref[0].astype(jnp.float32), 0.0)
    weigh(0, grp, own.astype(jnp.bfloat16))

    def place_diag(slot, chip_slot, a, b, at):
        for flip, block in ((0, a), (1, b)):
            q = (chip_slot * CORES + flip) * dr
            for k in range(plan.tiles):
                diag[q : q + dr, slot * cols + k * LANES : slot * cols + (k + 1) * LANES] = (
                    block[chip_slot, at + k * dr : at + (k + 1) * dr, :].astype(jnp.float32)
                )

    slot = 0
    for b, steps in enumerate(batches):
        if b == 0:
            for j in range(plan.chips):
                place_diag(0, j, mine[b], theirs[b], len(steps) * plan.message)
        for t, step in enumerate(steps):
            slot += 1
            at = t * plan.message
            for j in range(plan.chips):
                source = lax.bitwise_xor(chip, j)
                col, row = lax.rem(source, plan.col_cuts), lax.div(source, plan.col_cuts)
                for k in range(plan.wide):
                    a = mine[b][j, at + k * plan.piece : at + (k + 1) * plan.piece, :]
                    o = theirs[b][j, at + k * plan.piece : at + (k + 1) * plan.piece, :]
                    lane = pl.multiple_of(col * plan.width + k * LANES, LANES)
                    mine_at = pl.multiple_of(core * plan.half + row * plan.piece, plan.piece)
                    their_at = pl.multiple_of((1 - core) * plan.half + row * plan.piece, plan.piece)
                    state[pl.ds(mine_at, plan.piece), pl.ds(lane, LANES)] = a
                    state[pl.ds(their_at, plan.piece), pl.ds(lane, LANES)] = o
                place_diag(slot, j, mine[b], theirs[b], at + plan.live_rows)
            sector = lax.rem(grp + plan.groups - step, plan.groups)
            weigh(slot, sector, state[...])

    slab = lax.dot_general(
        weight[...].astype(jnp.bfloat16),
        diag[...].astype(jnp.bfloat16),
        (((1,), (1,)), ((), ())),
        preferred_element_type=jnp.float32,
    )
    total = slab.shape[1]
    lane = lax.broadcasted_iota(jnp.int32, slab.shape, 1)
    bit = 1
    while bit < plan.pairs:
        span = bit * dr
        up = jnp.concatenate([slab[:, span:], slab[:, :span]], axis=1)
        down = jnp.concatenate([slab[:, total - span :], slab[:, : total - span]], axis=1)
        swapped = jnp.where(lax.rem(lax.div(lane, span), 2) == 0, up, down)
        keep = lax.rem(lax.div(me, bit), 2) == 0
        slab = jnp.where(keep, slab, swapped)
        bit *= 2
    out_ref[...] = slab[: plan.own_pairs, :]


def slab_call(plan, batches, sector_rows, wave, ops, mine, theirs):
    total_q = plan.pairs * plan.diag_rows
    vmem = pl.BlockSpec(memory_space=pltpu.VMEM)
    return pl.pallas_call(
        functools.partial(slab_kernel, plan, batches),
        out_shape=jax.ShapeDtypeStruct((plan.own_pairs, total_q), jnp.float32),
        in_specs=[pl.BlockSpec(memory_space=pltpu.SMEM)] + [vmem] * (2 + 2 * len(batches)),
        out_specs=vmem,
        scratch_shapes=[
            pltpu.VMEM((plan.rows, plan.cols), jnp.bfloat16),
            pltpu.VMEM((total_q, plan.groups * plan.cols), jnp.float32),
            pltpu.VMEM((8, plan.groups * plan.cols), jnp.float32),
        ],
        name="slab",
    )(sector_rows, wave, ops, *mine, *theirs)


def local(mesh, sector_rows, wavefunction, left_ops, right_diag):
    pairs, groups = mesh.shape["pair"], mesh.shape["grp"]
    plan = Plan(pairs, groups, wavefunction, right_diag, left_ops)
    batches = plan.batches()

    def send(x, to):
        hops = []
        for p in range(pairs):
            for g in range(groups):
                q, h = to(p, g)
                hops.append((p * groups + g, q * groups + h))
        return lax.ppermute(x, BOTH, hops)

    own = cut(plan, sector_rows, wavefunction, right_diag)
    moved = {}
    for d in [d for steps in batches for d in steps]:
        moved[d] = send(own, lambda p, g: (p, (g + d) % groups))
    mine, theirs = [], []
    for b, steps in enumerate(batches):
        parts = [moved[d] for d in steps]
        if b == 0:
            parts.append(own[plan.live_rows :])
        packed = jnp.concatenate(parts, axis=0) if len(parts) > 1 else parts[0]
        got = [packed]
        for j in range(1, plan.chips):
            got.append(send(packed, lambda p, g: (p ^ (j * CORES), g)))
        stacked = jnp.stack(got)
        mine.append(stacked)
        theirs.append(send(stacked, lambda p, g: (p ^ 1, g)))
    return slab_call(plan, batches, sector_rows, wavefunction, left_ops, mine, theirs)


def solution(mesh):
    in_specs = (
        P(),
        P("grp", None, None),
        P(("pair", "grp"), None, None, None),
        P("pair", "grp", None),
    )
    out_specs = P(("pair", "grp"), None)
    return jax.shard_map(
        functools.partial(local, mesh), mesh=mesh, in_specs=in_specs, out_specs=out_specs, check_vma=False
    )
```
